512 devices in a mesh: seq: 32 (over z, core), head: 16 (over x, y).
Axes of the slice: x: 4, y: 4, z: 16, core: 2. Of those that a mesh axis runs over, the one named last changes fastest.
Arguments:
- queries: bfloat16 [32768, 16, 128], P(('seq', 'head')), may hold values from -6 to 6
- keys: bfloat16 [32768, 16, 128], P(('seq', 'head')), may hold values from -6 to 6
- values: bfloat16 [32768, 16, 128], P(('seq', 'head')), may hold values from -6 to 6
- log_decay: bfloat16 [32768, 16], P(('seq', 'head')), may hold values from -1 to 0
- beta: bfloat16 [32768, 16], P(('seq', 'head')), may hold values from 0.0099 to 0.6
- norm_gain: float32 [128], replicated, may hold values from 0.25 to 1.75
Outputs:
- normed_core: bfloat16 [32768, 16, 128], P(('seq', 'head'))
The draws below stay inside these ranges and needn't reach their ends.
All inputs are finite; a program needn't handle non-finite values.
Results may differ from the reference program's by a relative error of at most 0.013.
Values may be sent and summed in bfloat16 or wider, within the bound.
No kernel may reach another device: no remote copies, remote signals or barrier semaphores. Data moves between devices by JAX's collectives and lax.ppermute only.
A program may use at most 64 MiB of HBM per device.

```python
import jax
import jax.numpy as jnp
from jax import lax

H = 16
DK = 128
GROUP = 64
TOK_DEV = 64
DOCUMENT_TOKENS = 32768


def head_roles(key, quick_count):
    order = jax.random.permutation(jax.random.fold_in(key, 101), H)
    return order < quick_count


def draw_keys(key, part):
    sample_sequences = jax.random.split(jax.random.fold_in(key, 404), 2)
    shared = jax.random.normal(sample_sequences[0], (1, H, DK), jnp.float32)
    random_noise = jax.random.normal(sample_sequences[1], (DOCUMENT_TOKENS, H, DK), jnp.float32)
    strength = 0.8
    return jnp.clip(random_noise + strength * shared, -6.0, 6.0).astype(jnp.bfloat16)


def draw_log_decay(key, part):
    quick = head_roles(key, H // 2)
    sample_sequences = jax.random.split(jax.random.fold_in(key, 303), 6)
    slow_rate = jnp.exp(jax.random.uniform(sample_sequences[0], (H,), jnp.float32, jnp.log(0.05), jnp.log(0.5))) / DOCUMENT_TOKENS
    quick_rate = 1.0 / jax.random.uniform(sample_sequences[1], (H,), jnp.float32, 30.0, 50.0)
    decay_rates = jnp.where(quick, quick_rate, slow_rate)
    random_noise = jax.random.uniform(sample_sequences[2], (DOCUMENT_TOKENS, H), jnp.float32, 0.5, 2.0)
    blocks = jax.random.uniform(sample_sequences[3], (DOCUMENT_TOKENS // TOK_DEV, 1, H), jnp.float32, 0.5, 2.0)
    block_multiplier = jnp.broadcast_to(blocks, (DOCUMENT_TOKENS // TOK_DEV, TOK_DEV, H)).reshape(DOCUMENT_TOKENS, H)
    spike_probability = jax.random.uniform(sample_sequences[4], (DOCUMENT_TOKENS, 1), jnp.float32) < 3.0 / DOCUMENT_TOKENS
    spike_magnitude = jnp.log(jax.random.uniform(sample_sequences[5], (DOCUMENT_TOKENS, 1), jnp.float32, 0.5, 0.8))
    spike_events = jnp.where(spike_probability, spike_magnitude, 0.0)
    return (-decay_rates * random_noise * block_multiplier + spike_events).astype(jnp.bfloat16)


def draw_beta(key, part):
    quick = head_roles(key, H // 2)
    sample_sequences = jax.random.split(jax.random.fold_in(key, 202), 3)
    level = jnp.exp(jax.random.uniform(sample_sequences[0], (H,), jnp.float32, jnp.log(0.02), jnp.log(0.05)))
    random_noise = jax.random.uniform(sample_sequences[1], (DOCUMENT_TOKENS, H), jnp.float32, 0.5, 2.0)
    quick_beta = jax.random.uniform(sample_sequences[2], (DOCUMENT_TOKENS, H), jnp.float32, 0.05, 0.59)
    return jnp.where(quick, quick_beta, level * random_noise).astype(jnp.bfloat16)


def block_scale(key, dims, shards, low, top_value):
    factor_of, own = 1.0, jax.random.fold_in(key, 6)
    for axis_at, shards_of in shards:
        draws = jnp.exp(jax.random.uniform(jax.random.fold_in(own, axis_at), (shards_of,), jnp.float32, low / len(shards), top_value / len(shards)))
        factor_of = factor_of * jnp.repeat(draws, dims[axis_at] // shards_of).reshape([-1 if axis == axis_at else 1 for axis in range(len(dims))])
    return factor_of


def scatter_about(key, shape, scale, most, pieces=(), held_as=jnp.bfloat16):
    gain = block_scale(key, shape, pieces, -0.22, 0.18) if pieces else 1.0
    values = jax.random.normal(key, shape, jnp.float32) * scale * gain
    return jnp.minimum(jnp.maximum(values, -most), most).astype(held_as)


def setup_inputs(seed: int = 0) -> dict:
    seeds = jax.random.split(jax.random.key(seed), 7)
    queries = scatter_about(seeds[0], (DOCUMENT_TOKENS, H, DK), 1.0, 6.0, ((0, 512),))
    keys = draw_keys(jax.random.fold_in(seeds[6], 71), 0)
    values = scatter_about(seeds[2], (DOCUMENT_TOKENS, H, DK), 1.0, 6.0, ((0, 512),))
    log_decay = draw_log_decay(jax.random.fold_in(seeds[6], 71), 0)
    beta = draw_beta(jax.random.fold_in(seeds[6], 71), 0)
    norm_gain = jnp.clip(1.0 + 0.15 * jax.random.normal(seeds[5], (DK,), jnp.float32), 0.25, 1.75)
    return dict(queries=queries, keys=keys, values=values, log_decay=log_decay, beta=beta, norm_gain=norm_gain)


HIGH = lax.Precision.HIGHEST

def unit_rows(tensor):
    tensor = tensor.astype(jnp.float32)
    return tensor * lax.rsqrt(lax.optimization_barrier(jnp.sum(tensor * tensor, axis=-1, keepdims=True)) + 1e-06)

def key_terms(group_keys, group_values, group_gates, group_betas):
    cumulative = jnp.cumsum(group_gates, axis=-1)
    row_ids = lax.broadcasted_iota(jnp.int32, (GROUP, GROUP), 0)
    col_ids = lax.broadcasted_iota(jnp.int32, (GROUP, GROUP), 1)
    within = row_ids >= col_ids
    spread = jnp.where(within, jnp.exp(jnp.where(within, cumulative[..., :, None] - cumulative[..., None, :], 0.0)), 0.0)
    intersection = jnp.einsum('...id,...jd->...ij', group_keys, group_keys, precision=HIGH)
    lower_part = jnp.where(row_ids > col_ids, intersection * spread, 0.0) * group_betas[..., :, None]
    system = lower_part + jnp.eye(GROUP, dtype=jnp.float32)
    scaled = jnp.concatenate([group_values, group_keys * jnp.exp(cumulative)[..., None]], axis=-1) * group_betas[..., None]
    solved = jax.scipy.linalg.solve_triangular(system, scaled, lower=True, unit_diagonal=True)
    head_width = group_keys.shape[-1]
    pseudo = solved[..., :head_width]
    erasers = solved[..., head_width:]
    final_log = cumulative[..., -1:]
    carried = group_keys * jnp.exp(final_log - cumulative)[..., None]
    return (cumulative, spread, pseudo, erasers, carried, jnp.exp(final_log[..., 0]))

def reference(queries, keys, values, log_decay, beta, norm_gain):
    count = DOCUMENT_TOKENS // GROUP
    unit_q = (unit_rows(queries) * DK ** (-0.5)).astype(jnp.bfloat16)
    unit_k = unit_rows(keys).astype(jnp.bfloat16)

    def by_group(tensor):
        return tensor.astype(jnp.float32).reshape(count, GROUP, H, DK).transpose(0, 2, 1, 3)

    def gate_group(tensor):
        return tensor.astype(jnp.float32).reshape(count, GROUP, H).transpose(0, 2, 1)
    inputs_all = (by_group(unit_q), by_group(unit_k), by_group(values), gate_group(log_decay), gate_group(beta))

    def advance(state, inputs_one):
        group_q, group_k, group_v, group_g, group_b = inputs_one
        cumulative, spread, pseudo, erasers, carried, decays = key_terms(group_k, group_v, group_g, group_b)
        residue = pseudo - jnp.einsum('hcd,hde->hce', erasers, state, precision=HIGH)
        scores = jnp.einsum('hid,hjd->hij', group_q, group_k, precision=HIGH) * spread
        core = jnp.einsum('hcd,hde->hce', group_q * jnp.exp(cumulative)[..., None], state, precision=HIGH)
        core = core + jnp.einsum('hij,hje->hie', scores, residue, precision=HIGH)
        updated = decays[:, None, None] * state + jnp.einsum('hcd,hce->hde', carried, residue, precision=HIGH)
        return (updated, core)
    start = jnp.zeros((H, DK, DK), jnp.float32)
    _, cores = lax.scan(advance, start, inputs_all)
    core_rows = cores.transpose(0, 2, 1, 3).reshape(DOCUMENT_TOKENS, H, DK)
    scale_rows = lax.rsqrt(lax.optimization_barrier(jnp.mean(core_rows * core_rows, axis=-1, keepdims=True)) + 1e-06)
    return (core_rows * scale_rows * norm_gain).astype(jnp.bfloat16)
```

```python
import jax
import jax.numpy as jnp
from jax import lax
from jax.experimental import pallas as pl
from jax.experimental.pallas import tpu as pltpu
from jax.sharding import PartitionSpec as P

D = 128
TOK = 64
HEADS = 16
SLAB = TOK * HEADS
CHUNK = 128
CHUNKS = SLAB // CHUNK
KEY, VALUE, QUERY, GATE, ROWS = 0, 64, 128, 192, 200
F32, BF16 = jnp.float32, jnp.bfloat16
VMEM = pl.BlockSpec(memory_space=pltpu.VMEM)
SMEM = pl.BlockSpec(memory_space=pltpu.SMEM)


def mm(left, right):
    return jnp.dot(left, right, preferred_element_type=F32)


def mm_nt(left, right):
    return lax.dot_general(left, right, (((1,), (1,)), ((), ())), preferred_element_type=F32)


def mm_tn(left, right):
    return lax.dot_general(left, right, (((0,), (0,)), ((), ())), preferred_element_type=F32)


def split(value):
    high = value.astype(BF16)
    return high, (value - high.astype(F32)).astype(BF16)


def wide(value):
    return jnp.concatenate(split(value), axis=1)


def tall(value):
    return jnp.concatenate(split(value), axis=0)


def twice(value, axis):
    return jnp.concatenate([value, value], axis=axis)


def square(value):
    high, low = split(value)
    top = jnp.concatenate([high, low], axis=1)
    bottom = jnp.concatenate([high, jnp.zeros_like(high)], axis=1)
    return jnp.concatenate([top, bottom], axis=0)


def halves(value):
    return value[:, :D] + value[:, D:]


def mm3(left, right):
    return halves(mm(wide(left), square(right)))


def mm3_wide(left, right):
    high, low = split(right)
    left_high, left_low = split(left)
    both = jnp.concatenate([left_high, left_low], axis=1)
    return mm(both, twice(high, 0)) + mm(left_high, low)


def iotas(rows, columns):
    shape = (rows, columns)
    return lax.broadcasted_iota(jnp.int32, shape, 0), lax.broadcasted_iota(jnp.int32, shape, 1)


def ones_where(condition):
    return jnp.where(condition, 1.0, 0.0).astype(BF16)


def gates(received):
    rows = received[:, GATE:ROWS, :].astype(F32)[:, 0, :].astype(BF16)
    chunk_ids, source_ids = iotas(CHUNKS, HEADS)
    even = mm(ones_where(source_ids == 2 * chunk_ids), rows).astype(BF16)
    odd = mm(ones_where(source_ids == 2 * chunk_ids + 1), rows).astype(BF16)
    to, at = iotas(CHUNK, D)
    sum_even = ones_where((at < TOK) & (at <= to))
    sum_odd = ones_where((at < TOK) & (at + TOK <= to))
    beta_even = ones_where((to < TOK) & (at == to + TOK))
    beta_odd = ones_where((to >= TOK) & (at == to))
    log_rows = mm_nt(even, sum_even) + mm_nt(odd, sum_odd)
    log_columns = mm_nt(sum_even, even) + mm_nt(sum_odd, odd)
    beta_rows = mm_nt(even, beta_even) + mm_nt(odd, beta_odd)
    beta_columns = mm_nt(beta_even, even) + mm_nt(beta_odd, odd)
    return log_rows, log_columns, beta_rows, beta_columns


def part(received, chunk, offset):
    return received[2 * chunk : 2 * chunk + 2, offset : offset + TOK, :].reshape(CHUNK, D)


def spread_of(log_rows, log_columns, chunk, row_ids, column_ids):
    difference = log_columns[:, chunk : chunk + 1] - log_rows[chunk : chunk + 1, :]
    return jnp.exp(jnp.where(row_ids >= column_ids, difference, -1e30))


def pack_kernel(queries, keys, values, log_decay, beta, sent, key_rows, value_rows, query_rows):
    wide_keys = keys[...].reshape(SLAB, D).astype(F32)
    total = jnp.sum(wide_keys * wide_keys, axis=1, keepdims=True)
    key_rows[...] = wide_keys * lax.rsqrt(total + 1e-06)
    value_rows[...] = values[...].reshape(SLAB, D).astype(F32)
    query_rows[...] = queries[...].reshape(SLAB, D).astype(F32)
    to, at = iotas(TOK, D)
    rows = mm_tn(log_decay[...], ones_where(at == to)) + mm_tn(beta[...], ones_where(at == to + TOK))
    for head in range(HEADS):
        pick = pl.ds(head, TOK, stride=HEADS)
        sent[head, KEY : KEY + TOK, :] = key_rows[pick, :].astype(BF16)
        sent[head, VALUE : VALUE + TOK, :] = value_rows[pick, :].astype(BF16)
        sent[head, QUERY : QUERY + TOK, :] = query_rows[pick, :].astype(BF16)
        sent[head, GATE:ROWS, :] = jnp.broadcast_to(rows[head : head + 1, :], (8, D)).astype(BF16)


def map_kernel(received, sent, prefixes, solved):
    log_rows, log_columns, beta_rows, beta_columns = gates(received)
    row_ids, column_ids = iotas(CHUNK, CHUNK)
    apart = row_ids ^ column_ids
    eye = jnp.where(apart == 0, 1.0, 0.0)
    lowers, inverses = [], []
    for c in range(CHUNKS):
        keys = part(received, c, KEY)
        spread = spread_of(log_rows, log_columns, c, row_ids, column_ids)
        lower = jnp.where(row_ids > column_ids, mm_nt(keys, keys) * spread, 0.0)
        lower = lower * beta_columns[:, c : c + 1]
        lowers.append(lower)
        inverses.append(eye - jnp.where(apart == 1, lower, 0.0))
    for level in range(1, 7):
        mask = (apart >> level) == 1
        for c in range(CHUNKS):
            inverse = inverses[c]
            inner = mm3(inverse, jnp.where(mask, lowers[c], 0.0))
            inverses[c] = inverse - mm3(inner, inverse)
    log_scale = jnp.exp(log_rows)
    prefix = None
    for c in range(CHUNKS):
        keys, values = part(received, c, KEY), part(received, c, VALUE)
        inverse = inverses[c] * beta_rows[c : c + 1, :]
        erasers = mm(wide(inverse * log_scale[c : c + 1, :]), twice(keys, 0))
        pseudo = mm(wide(inverse), twice(values, 0))
        both = jnp.concatenate([erasers, pseudo], axis=1)
        solved[c] = both
        last = log_rows[c : c + 1, CHUNK - 1 : CHUNK]
        carried = both * jnp.exp(last - log_columns[:, c : c + 1])
        maps = mm_tn(twice(keys, 0), tall(carried))
        linear = eye * jnp.exp(last) - maps[:, :D]
        offset = maps[:, D:]
        if prefix is None:
            prefixes[c] = jnp.concatenate([eye, jnp.zeros_like(eye)], axis=1)
            prefix = jnp.concatenate([linear, offset], axis=1)
        else:
            prefixes[c] = prefix
            moved = mm3_wide(linear, prefix)
            prefix = jnp.concatenate([moved[:, :D], moved[:, D:] + offset], axis=1)
    for copy in range(4):
        sent[copy] = prefix.astype(BF16)


def query_kernel(received, prefixes, solved, query_maps, base):
    log_rows, log_columns, _, _ = gates(received)
    row_ids, column_ids = iotas(CHUNK, CHUNK)
    for c in range(CHUNKS):
        keys = part(received, c, KEY)
        raw = part(received, c, QUERY).astype(F32)
        total = jnp.sum(raw * raw, axis=1, keepdims=True)
        queries = (raw * lax.rsqrt(total + 1e-06) * D**-0.5).astype(BF16)
        spread = spread_of(log_rows, log_columns, c, row_ids, column_ids)
        scores = mm_nt(queries, keys) * spread
        prefix, both = prefixes[c], solved[c]
        erased = mm3_wide(both[:, :D], prefix)
        residue = jnp.concatenate([-erased[:, :D], both[:, D:] - erased[:, D:]], axis=1)
        direct = mm(twice(queries, 1), tall(prefix)) * jnp.exp(log_columns[:, c : c + 1])
        result = direct + mm3_wide(scores, residue)
        query_maps[c * CHUNK : (c + 1) * CHUNK, :] = wide(result[:, :D])
        base[c * CHUNK : (c + 1) * CHUNK, :] = result[:, D:]


def block_kernel(place, received, before, total):
    eye = jnp.where(jnp.equal(*iotas(D, D)), 1.0, 0.0)
    prefix = jnp.concatenate([eye, jnp.zeros_like(eye)], axis=1)
    chosen = prefix
    for p in range(4):
        if p:
            chosen = jnp.where(place[0] == p, prefix, chosen)
        linear = received[p, :, :D]
        if p == 0:
            prefix = received[p].astype(F32)
        else:
            moved = mm(twice(linear, 1), tall(prefix))
            offset = received[p, :, D:].astype(F32)
            prefix = jnp.concatenate([moved[:, :D], moved[:, D:] + offset], axis=1)
    before[...] = chosen
    total[...] = prefix.astype(BF16)


def join_kernel(total, earlier, joined):
    moved = mm(total[:, :D], earlier[...])
    joined[:, :D] = moved[:, :D].astype(BF16)
    joined[:, D:] = (moved[:, D:] + total[:, D:].astype(F32)).astype(BF16)


def shift_kernel(before, earlier, query_maps, base, shifted_maps, shifted_base):
    first = before[...]
    moved = mm(wide(first[:, :D]), twice(earlier[...], 0))
    prefix = jnp.concatenate([moved[:, :D], moved[:, D:] + first[:, D:]], axis=1)
    high, low = split(prefix)
    for c in range(4):
        rows = slice(c * 256, (c + 1) * 256)
        maps = query_maps[rows, :]
        result = mm(maps, twice(high, 0)) + mm(maps[:, :D], low)
        shifted_maps[rows, :] = wide(result[:, :D])
        shifted_base[rows, :] = base[rows, :] + result[:, D:]


def output_kernel(near, far, farthest, query_maps, base, gain, sent):
    state = farthest[...].astype(F32)
    state = mm(twice(far[:, :D], 1), tall(state)) + far[:, D:].astype(F32)
    state = mm(twice(near[:, :D], 1), tall(state)) + near[:, D:].astype(F32)
    weights = square(state)
    for c in range(4):
        rows = slice(c * 256, (c + 1) * 256)
        core = halves(mm(query_maps[rows, :], weights)) + base[rows, :]
        scale = lax.rsqrt(jnp.mean(core * core, axis=1, keepdims=True) + 1e-06)
        sent[rows, :] = (core * scale * gain[...]).astype(BF16)


def unpack_kernel(received, out, rows):
    rows[...] = received[...].reshape(SLAB, D).astype(F32)
    for token in range(TOK):
        out[token] = rows[pl.ds(token, HEADS, stride=TOK), :].astype(BF16)


def call(kernel, outs, *operands, scratch=(), flops=0, scalars=0):
    outs = [jax.ShapeDtypeStruct(shape, dtype) for shape, dtype in outs]
    size = sum(a.size * a.dtype.itemsize for a in operands)
    return pl.pallas_call(
        kernel,
        out_shape=outs if len(outs) > 1 else outs[0],
        in_specs=[SMEM] * scalars + [VMEM] * (len(operands) - scalars),
        out_specs=[VMEM] * len(outs) if len(outs) > 1 else VMEM,
        scratch_shapes=scratch,
        compiler_params=pltpu.CompilerParams(vmem_limit_bytes=24 << 20),
        cost_estimate=pl.CostEstimate(flops=flops, bytes_accessed=size, transcendentals=0),
        name=kernel.__name__,
    )(*operands)


def local(queries, keys, values, log_decay, beta, norm_gain):
    rows = pltpu.VMEM((SLAB, D), F32)
    packed = call(
        pack_kernel,
        [((HEADS, ROWS, D), BF16)],
        queries,
        keys,
        values,
        log_decay,
        beta,
        scratch=[rows, rows, rows],
    )
    received = lax.all_to_all(packed, "head", 0, 0, tiled=True)
    maps, prefixes, solved = call(
        map_kernel,
        [((4, D, 2 * D), BF16), ((CHUNKS, D, 2 * D), F32), ((CHUNKS, CHUNK, 2 * D), F32)],
        received,
        flops=1 << 33,
    )
    count = lax.axis_size("seq")
    groups = [[first + p for p in range(4)] for first in range(0, count, 4)]
    block = lax.all_to_all(maps, "seq", 0, 0, axis_index_groups=groups, tiled=True)
    query_maps, base = call(
        query_kernel,
        [((SLAB, 2 * D), BF16), ((SLAB, D), F32)],
        received,
        prefixes,
        solved,
        flops=1 << 33,
    )
    place = (lax.axis_index("seq") % 4).astype(jnp.int32).reshape(1)
    before, total = call(
        block_kernel, [((D, 2 * D), F32), ((D, 2 * D), BF16)], place, block, scalars=1
    )

    def moved(value, by):
        return lax.ppermute(value, "seq", [(s, s + by) for s in range(count - by)])

    earlier = moved(total, 4)
    joined = call(join_kernel, [((D, 2 * D), BF16)], total, earlier)
    near, far, farthest = moved(joined, 8), moved(joined, 16), moved(joined[:, D:], 24)
    query_maps, base = call(
        shift_kernel,
        [((SLAB, 2 * D), BF16), ((SLAB, D), F32)],
        before,
        earlier,
        query_maps,
        base,
        flops=1 << 31,
    )
    normed = call(
        output_kernel,
        [((SLAB, D), BF16)],
        near,
        far,
        farthest,
        query_maps,
        base,
        norm_gain.reshape(1, D),
    )
    returned = lax.all_to_all(normed.reshape(HEADS, TOK, D), "head", 0, 0, tiled=True)
    return call(unpack_kernel, [((TOK, HEADS, D), BF16)], returned, scratch=[rows])


def solution(mesh):
    rows = P(("seq", "head"), None, None)
    columns = P(("seq", "head"), None)
    return jax.shard_map(
        local,
        mesh=mesh,
        in_specs=(rows, rows, rows, columns, columns, P()),
        out_specs=rows,
        check_vma=False,
    )
```

```python
import jax
import jax.numpy as jnp
from jax import lax
from jax.experimental import pallas as pl
from jax.experimental.pallas import tpu as pltpu
from jax.sharding import PartitionSpec as P


D = 128
TOK = 64
HEADS = 16
SLAB = TOK * HEADS
CHUNK = 128
CHUNKS = SLAB // CHUNK
KEY, VALUE, QUERY, GATE, ROWS = 0, 64, 128, 192, 200
F32, BF16 = jnp.float32, jnp.bfloat16
VMEM = pl.BlockSpec(memory_space=pltpu.VMEM)
SMEM = pl.BlockSpec(memory_space=pltpu.SMEM)


def mm(left, right):
    return jnp.dot(left, right, preferred_element_type=F32)


def mm_nt(left, right):
    return lax.dot_general(left, right, (((1,), (1,)), ((), ())), preferred_element_type=F32)


def mm_tn(left, right):
    return lax.dot_general(left, right, (((0,), (0,)), ((), ())), preferred_element_type=F32)


def split(value):
    high = value.astype(BF16)
    return high, (value - high.astype(F32)).astype(BF16)


def wide(value):
    return jnp.concatenate(split(value), axis=1)


def tall(value):
    return jnp.concatenate(split(value), axis=0)


def twice(value, axis):
    return jnp.concatenate([value, value], axis=axis)


def square(value):
    high, low = split(value)
    top = jnp.concatenate([high, low], axis=1)
    bottom = jnp.concatenate([high, jnp.zeros_like(high)], axis=1)
    return jnp.concatenate([top, bottom], axis=0)


def halves(value):
    return value[:, :D] + value[:, D:]


def mm3(left, right):
    return halves(mm(wide(left), square(right)))


def mm3_wide(left, right):
    high, low = split(right)
    left_high, left_low = split(left)
    both = jnp.concatenate([left_high, left_low], axis=1)
    return mm(both, twice(high, 0)) + mm(left_high, low)


def iotas(rows, columns):
    shape = (rows, columns)
    return lax.broadcasted_iota(jnp.int32, shape, 0), lax.broadcasted_iota(jnp.int32, shape, 1)


def ones_where(condition):
    return jnp.where(condition, 1.0, 0.0).astype(BF16)


def gates(received):
    rows = received[:, GATE:ROWS, :].astype(F32)[:, 0, :].astype(BF16)
    chunk_ids, source_ids = iotas(CHUNKS, HEADS)
    even = mm(ones_where(source_ids == 2 * chunk_ids), rows).astype(BF16)
    odd = mm(ones_where(source_ids == 2 * chunk_ids + 1), rows).astype(BF16)
    to, at = iotas(CHUNK, D)
    sum_even = ones_where((at < TOK) & (at <= to))
    sum_odd = ones_where((at < TOK) & (at + TOK <= to))
    beta_even = ones_where((to < TOK) & (at == to + TOK))
    beta_odd = ones_where((to >= TOK) & (at == to))
    log_rows = mm_nt(even, sum_even) + mm_nt(odd, sum_odd)
    log_columns = mm_nt(sum_even, even) + mm_nt(sum_odd, odd)
    beta_rows = mm_nt(even, beta_even) + mm_nt(odd, beta_odd)
    beta_columns = mm_nt(beta_even, even) + mm_nt(beta_odd, odd)
    return log_rows, log_columns, beta_rows, beta_columns


def part(received, chunk, offset):
    return received[2 * chunk : 2 * chunk + 2, offset : offset + TOK, :].reshape(CHUNK, D)


def spread_of(log_rows, log_columns, chunk, row_ids, column_ids):
    difference = log_columns[:, chunk : chunk + 1] - log_rows[chunk : chunk + 1, :]
    return jnp.exp(jnp.where(row_ids >= column_ids, difference, -1e30))


def pack_kernel(*refs):
    sources, (sent, gains, taken, decays, betas, rows, arrived) = refs[:6], refs[6:]
    targets = (decays, betas, gains, taken.at[0], taken.at[1], taken.at[2])
    copies = [
        pltpu.make_async_copy(source, target, arrived.at[n])
        for n, (source, target) in enumerate(zip(sources, targets))
    ]
    for copy in copies:
        copy.start()
    for copy in copies[:3]:
        copy.wait()
    to, at = iotas(TOK, D)
    gate_rows = mm(decays[...], ones_where(at == to)) + mm(betas[...], ones_where(at == to + TOK))
    for head in range(HEADS):
        sent[head, GATE:ROWS, :] = jnp.broadcast_to(gate_rows[head : head + 1, :], (8, D)).astype(BF16)
    for n, offset in enumerate((KEY, VALUE, QUERY)):
        copies[3 + n].wait()
        raw = taken[n].reshape(SLAB, D).astype(F32)
        if n == 0:
            raw = raw * lax.rsqrt(jnp.sum(raw * raw, axis=1, keepdims=True) + 1e-06)
        rows[n] = raw
        for head in range(HEADS):
            picked = rows[n, pl.ds(head, TOK, stride=HEADS), :]
            sent[head, offset : offset + TOK, :] = picked.astype(BF16)


def map_kernel(received, sent, prefixes, solved):
    log_rows, log_columns, beta_rows, beta_columns = gates(received)
    row_ids, column_ids = iotas(CHUNK, CHUNK)
    apart = row_ids ^ column_ids
    eye = jnp.where(apart == 0, 1.0, 0.0)
    lowers, inverses = [], []
    for c in range(CHUNKS):
        keys = part(received, c, KEY)
        spread = spread_of(log_rows, log_columns, c, row_ids, column_ids)
        lower = jnp.where(row_ids > column_ids, mm_nt(keys, keys) * spread, 0.0)
        lower = lower * beta_columns[:, c : c + 1]
        lowers.append(lower)
        inverses.append(eye - jnp.where(apart == 1, lower, 0.0))
    for level in range(1, 7):
        mask = (apart >> level) == 1
        for c in range(CHUNKS):
            inverse = inverses[c]
            inner = mm3(inverse, jnp.where(mask, lowers[c], 0.0))
            inverses[c] = inverse - mm3(inner, inverse)
    log_scale = jnp.exp(log_rows)
    prefix = None
    for c in range(CHUNKS):
        keys, values = part(received, c, KEY), part(received, c, VALUE)
        inverse = inverses[c] * beta_rows[c : c + 1, :]
        erasers = mm(wide(inverse * log_scale[c : c + 1, :]), twice(keys, 0))
        pseudo = mm(wide(inverse), twice(values, 0))
        both = jnp.concatenate([erasers, pseudo], axis=1)
        solved[c] = both
        last = log_rows[c : c + 1, CHUNK - 1 : CHUNK]
        carried = both * jnp.exp(last - log_columns[:, c : c + 1])
        maps = mm_tn(twice(keys, 0), tall(carried))
        linear = eye * jnp.exp(last) - maps[:, :D]
        offset = maps[:, D:]
        if prefix is None:
            prefixes[c] = jnp.concatenate([eye, jnp.zeros_like(eye)], axis=1)
            prefix = jnp.concatenate([linear, offset], axis=1)
        else:
            prefixes[c] = prefix
            moved = mm3_wide(linear, prefix)
            prefix = jnp.concatenate([moved[:, :D], moved[:, D:] + offset], axis=1)
    for copy in range(4):
        sent[copy] = prefix.astype(BF16)


def query_kernel(received, prefixes, solved, query_maps, base):
    log_rows, log_columns, _, _ = gates(received)
    row_ids, column_ids = iotas(CHUNK, CHUNK)
    for c in range(CHUNKS):
        keys = part(received, c, KEY)
        raw = part(received, c, QUERY).astype(F32)
        total = jnp.sum(raw * raw, axis=1, keepdims=True)
        queries = (raw * lax.rsqrt(total + 1e-06) * D**-0.5).astype(BF16)
        spread = spread_of(log_rows, log_columns, c, row_ids, column_ids)
        scores = mm_nt(queries, keys) * spread
        prefix, both = prefixes[c], solved[c]
        erased = mm3_wide(both[:, :D], prefix)
        residue = jnp.concatenate([-erased[:, :D], both[:, D:] - erased[:, D:]], axis=1)
        direct = mm(twice(queries, 1), tall(prefix)) * jnp.exp(log_columns[:, c : c + 1])
        result = direct + mm3_wide(scores, residue)
        query_maps[c * CHUNK : (c + 1) * CHUNK, :] = wide(result[:, :D])
        base[c * CHUNK : (c + 1) * CHUNK, :] = result[:, D:]


def block_kernel(place, received, before, total):
    eye = jnp.where(jnp.equal(*iotas(D, D)), 1.0, 0.0)
    prefix = jnp.concatenate([eye, jnp.zeros_like(eye)], axis=1)
    chosen = prefix
    for p in range(4):
        if p:
            chosen = jnp.where(place[0] == p, prefix, chosen)
        linear = received[p, :, :D]
        if p == 0:
            prefix = received[p].astype(F32)
        else:
            moved = mm(twice(linear, 1), tall(prefix))
            offset = received[p, :, D:].astype(F32)
            prefix = jnp.concatenate([moved[:, :D], moved[:, D:] + offset], axis=1)
    before[...] = chosen
    total[...] = prefix.astype(BF16)


def join_kernel(total, earlier, joined):
    moved = mm(total[:, :D], earlier[...])
    joined[:, :D] = moved[:, :D].astype(BF16)
    joined[:, D:] = (moved[:, D:] + total[:, D:].astype(F32)).astype(BF16)


def shift_kernel(before, earlier, query_maps, base, shifted_maps, shifted_base):
    first = before[...]
    moved = mm(wide(first[:, :D]), twice(earlier[...], 0))
    prefix = jnp.concatenate([moved[:, :D], moved[:, D:] + first[:, D:]], axis=1)
    high, low = split(prefix)
    for c in range(4):
        rows = slice(c * 256, (c + 1) * 256)
        maps = query_maps[rows, :]
        result = mm(maps, twice(high, 0)) + mm(maps[:, :D], low)
        shifted_maps[rows, :] = wide(result[:, :D])
        shifted_base[rows, :] = base[rows, :] + result[:, D:]


def output_kernel(near, far, farthest, query_maps, base, gain, sent):
    state = farthest[...].astype(F32)
    state = mm(twice(far[:, :D], 1), tall(state)) + far[:, D:].astype(F32)
    state = mm(twice(near[:, :D], 1), tall(state)) + near[:, D:].astype(F32)
    weights = square(state)
    for c in range(4):
        rows = slice(c * 256, (c + 1) * 256)
        core = halves(mm(query_maps[rows, :], weights)) + base[rows, :]
        scale = lax.rsqrt(jnp.mean(core * core, axis=1, keepdims=True) + 1e-06)
        sent[rows, :] = (core * scale * gain[...]).astype(BF16)


def unpack_kernel(received, out, rows):
    rows[...] = received[...].reshape(SLAB, D).astype(F32)
    for token in range(TOK):
        out[token] = rows[pl.ds(token, HEADS, stride=TOK), :].astype(BF16)


def call(kernel, outs, *operands, scratch=(), flops=0, scalars=0, raw=0):
    outs = [jax.ShapeDtypeStruct(shape, dtype) for shape, dtype in outs]
    size = sum(a.size * a.dtype.itemsize for a in operands)
    return pl.pallas_call(
        kernel,
        out_shape=outs if len(outs) > 1 else outs[0],
        in_specs=[SMEM] * scalars
        + [pl.BlockSpec(memory_space=pltpu.HBM)] * raw
        + [VMEM] * (len(operands) - scalars - raw),
        out_specs=[VMEM] * len(outs) if len(outs) > 1 else VMEM,
        scratch_shapes=scratch,
        compiler_params=pltpu.CompilerParams(vmem_limit_bytes=24 << 20),
        cost_estimate=pl.CostEstimate(flops=flops, bytes_accessed=size, transcendentals=0),
    )(*operands)


def local(queries, keys, values, log_decay, beta, norm_gain):
    sources = (log_decay.T, beta.T, norm_gain.reshape(1, D), keys, values, queries)
    packed, gains = call(
        pack_kernel,
        [((HEADS, ROWS, D), BF16), ((1, D), F32)],
        *(pltpu.with_memory_space_constraint(source, pltpu.HBM) for source in sources),
        scratch=[
            pltpu.VMEM((3, TOK, HEADS, D), BF16),
            pltpu.VMEM((HEADS, TOK), BF16),
            pltpu.VMEM((HEADS, TOK), BF16),
            pltpu.VMEM((3, SLAB, D), F32),
            pltpu.SemaphoreType.DMA((6,)),
        ],
        raw=6,
    )
    received = lax.all_to_all(packed, "head", 0, 0, tiled=True)
    maps, prefixes, solved = call(
        map_kernel,
        [((4, D, 2 * D), BF16), ((CHUNKS, D, 2 * D), F32), ((CHUNKS, CHUNK, 2 * D), F32)],
        received,
        flops=1 << 33,
    )
    count = lax.axis_size("seq")
    groups = [[first + p for p in range(4)] for first in range(0, count, 4)]
    block = lax.all_to_all(maps, "seq", 0, 0, axis_index_groups=groups, tiled=True)
    query_maps, base = call(
        query_kernel,
        [((SLAB, 2 * D), BF16), ((SLAB, D), F32)],
        received,
        prefixes,
        solved,
        flops=1 << 33,
    )
    place = (lax.axis_index("seq") % 4).astype(jnp.int32).reshape(1)
    before, total = call(
        block_kernel, [((D, 2 * D), F32), ((D, 2 * D), BF16)], place, block, scalars=1
    )

    def moved(value, by):
        return lax.ppermute(value, "seq", [(s, s + by) for s in range(count - by)])

    earlier = moved(total, 4)
    joined = call(join_kernel, [((D, 2 * D), BF16)], total, earlier)
    near = moved(joined, 8)
    far = lax.ppermute(joined, "seq", [(s, (s ^ 2) + 16) for s in range(count - 16)])
    farthest = moved(joined[:, D:], 24)
    query_maps, base = call(
        shift_kernel,
        [((SLAB, 2 * D), BF16), ((SLAB, D), F32)],
        before,
        earlier,
        query_maps,
        base,
        flops=1 << 31,
    )
    normed = call(
        output_kernel,
        [((SLAB, D), BF16)],
        near,
        far,
        farthest,
        query_maps,
        base,
        gains,
    )
    returned = lax.all_to_all(normed.reshape(HEADS, TOK, D), "head", 0, 0, tiled=True)
    return call(unpack_kernel, [((TOK, HEADS, D), BF16)], returned, scratch=[pltpu.VMEM((SLAB, D), F32)])


def solution(mesh):
    rows = P(("seq", "head"), None, None)
    columns = P(("seq", "head"), None)
    return jax.shard_map(
        local,
        mesh=mesh,
        in_specs=(rows, rows, rows, columns, columns, P()),
        out_specs=rows,
        check_vma=False,
    )
```

```python
import jax
import jax.numpy as jnp
from jax import lax
from jax.experimental import pallas as pl
from jax.experimental.pallas import tpu as pltpu
from jax.sharding import PartitionSpec as P


D = 128
TOK = 64
HEADS = 16
SLAB = TOK * HEADS
CHUNK = 128
CHUNKS = SLAB // CHUNK
KEY, VALUE, QUERY, GATE, ROWS = 0, 64, 128, 192, 200
F32, BF16 = jnp.float32, jnp.bfloat16
VMEM = pl.BlockSpec(memory_space=pltpu.VMEM)
SMEM = pl.BlockSpec(memory_space=pltpu.SMEM)


def mm(left, right):
    return jnp.dot(left, right, preferred_element_type=F32)


def mm_nt(left, right):
    return lax.dot_general(left, right, (((1,), (1,)), ((), ())), preferred_element_type=F32)


def mm_tn(left, right):
    return lax.dot_general(left, right, (((0,), (0,)), ((), ())), preferred_element_type=F32)


def split(value):
    high = value.astype(BF16)
    return high, (value - high.astype(F32)).astype(BF16)


def wide(value):
    return jnp.concatenate(split(value), axis=1)


def tall(value):
    return jnp.concatenate(split(value), axis=0)


def twice(value, axis):
    return jnp.concatenate([value, value], axis=axis)


def square(value):
    high, low = split(value)
    top = jnp.concatenate([high, low], axis=1)
    bottom = jnp.concatenate([high, jnp.zeros_like(high)], axis=1)
    return jnp.concatenate([top, bottom], axis=0)


def halves(value):
    return value[:, :D] + value[:, D:]


def mm3(left, right):
    return halves(mm(wide(left), square(right)))


def mm3_wide(left, right):
    high, low = split(right)
    left_high, left_low = split(left)
    both = jnp.concatenate([left_high, left_low], axis=1)
    return mm(both, twice(high, 0)) + mm(left_high, low)


def iotas(rows, columns):
    shape = (rows, columns)
    return lax.broadcasted_iota(jnp.int32, shape, 0), lax.broadcasted_iota(jnp.int32, shape, 1)


def ones_where(condition):
    return jnp.where(condition, 1.0, 0.0).astype(BF16)


def gates(received):
    rows = received[:, GATE:ROWS, :].astype(F32)[:, 0, :].astype(BF16)
    chunk_ids, source_ids = iotas(CHUNKS, HEADS)
    even = mm(ones_where(source_ids == 2 * chunk_ids), rows).astype(BF16)
    odd = mm(ones_where(source_ids == 2 * chunk_ids + 1), rows).astype(BF16)
    to, at = iotas(CHUNK, D)
    sum_even = ones_where((at < TOK) & (at <= to))
    sum_odd = ones_where((at < TOK) & (at + TOK <= to))
    beta_even = ones_where((to < TOK) & (at == to + TOK))
    beta_odd = ones_where((to >= TOK) & (at == to))
    log_rows = mm_nt(even, sum_even) + mm_nt(odd, sum_odd)
    log_columns = mm_nt(sum_even, even) + mm_nt(sum_odd, odd)
    beta_rows = mm_nt(even, beta_even) + mm_nt(odd, beta_odd)
    beta_columns = mm_nt(beta_even, even) + mm_nt(beta_odd, odd)
    return log_rows, log_columns, beta_rows, beta_columns


def part(received, chunk, offset):
    return received[2 * chunk : 2 * chunk + 2, offset : offset + TOK, :].reshape(CHUNK, D)


def spread_of(log_rows, log_columns, chunk, row_ids, column_ids):
    difference = log_columns[:, chunk : chunk + 1] - log_rows[chunk : chunk + 1, :]
    return jnp.exp(jnp.where(row_ids >= column_ids, difference, -1e30))


def pack_kernel(*refs):
    sources, (sent, gains, taken, decays, betas, rows, arrived) = refs[:6], refs[6:]
    targets = (decays, betas, gains, taken.at[0], taken.at[1], taken.at[2])
    copies = [
        pltpu.make_async_copy(source, target, arrived.at[n])
        for n, (source, target) in enumerate(zip(sources, targets))
    ]
    for copy in copies:
        copy.start()
    for copy in copies[:3]:
        copy.wait()
    to, at = iotas(TOK, D)
    gate_rows = mm(decays[...], ones_where(at == to)) + mm(betas[...], ones_where(at == to + TOK))
    for head in range(HEADS):
        sent[head, GATE:ROWS, :] = jnp.broadcast_to(gate_rows[head : head + 1, :], (8, D)).astype(BF16)
    for n, offset in enumerate((KEY, VALUE, QUERY)):
        copies[3 + n].wait()
        raw = taken[n].reshape(SLAB, D).astype(F32)
        if n == 0:
            raw = raw * lax.rsqrt(jnp.sum(raw * raw, axis=1, keepdims=True) + 1e-06)
        rows[n] = raw
        for head in range(HEADS):
            picked = rows[n, pl.ds(head, TOK, stride=HEADS), :]
            sent[head, offset : offset + TOK, :] = picked.astype(BF16)


def map_kernel(received, sent, prefixes, solved):
    log_rows, log_columns, beta_rows, beta_columns = gates(received)
    row_ids, column_ids = iotas(CHUNK, CHUNK)
    apart = row_ids ^ column_ids
    eye = jnp.where(apart == 0, 1.0, 0.0)
    lowers, inverses = [], []
    for c in range(CHUNKS):
        keys = part(received, c, KEY)
        spread = spread_of(log_rows, log_columns, c, row_ids, column_ids)
        lower = jnp.where(row_ids > column_ids, mm_nt(keys, keys) * spread, 0.0)
        lower = lower * beta_columns[:, c : c + 1]
        lowers.append(lower)
        inverses.append(eye - jnp.where(apart == 1, lower, 0.0))
    for level in range(1, 7):
        mask = (apart >> level) == 1
        for c in range(CHUNKS):
            inverse = inverses[c]
            inner = mm3(inverse, jnp.where(mask, lowers[c], 0.0))
            inverses[c] = inverse - mm3(inner, inverse)
    log_scale = jnp.exp(log_rows)
    prefix = None
    for c in range(CHUNKS):
        keys, values = part(received, c, KEY), part(received, c, VALUE)
        inverse = inverses[c] * beta_rows[c : c + 1, :]
        erasers = mm(wide(inverse * log_scale[c : c + 1, :]), twice(keys, 0))
        pseudo = mm(wide(inverse), twice(values, 0))
        both = jnp.concatenate([erasers, pseudo], axis=1)
        solved[c] = both
        last = log_rows[c : c + 1, CHUNK - 1 : CHUNK]
        carried = both * jnp.exp(last - log_columns[:, c : c + 1])
        maps = mm_tn(twice(keys, 0), tall(carried))
        linear = eye * jnp.exp(last) - maps[:, :D]
        offset = maps[:, D:]
        if prefix is None:
            prefixes[c] = jnp.concatenate([eye, jnp.zeros_like(eye)], axis=1)
            prefix = jnp.concatenate([linear, offset], axis=1)
        else:
            prefixes[c] = prefix
            moved = mm3_wide(linear, prefix)
            prefix = jnp.concatenate([moved[:, :D], moved[:, D:] + offset], axis=1)
    sent[...] = prefix.astype(BF16)


def query_kernel(received, prefixes, solved, query_maps, base):
    log_rows, log_columns, _, _ = gates(received)
    row_ids, column_ids = iotas(CHUNK, CHUNK)
    for c in range(CHUNKS):
        keys = part(received, c, KEY)
        raw = part(received, c, QUERY).astype(F32)
        total = jnp.sum(raw * raw, axis=1, keepdims=True)
        queries = (raw * lax.rsqrt(total + 1e-06) * D**-0.5).astype(BF16)
        spread = spread_of(log_rows, log_columns, c, row_ids, column_ids)
        scores = mm_nt(queries, keys) * spread
        prefix, both = prefixes[c], solved[c]
        erased = mm3_wide(both[:, :D], prefix)
        residue = jnp.concatenate([-erased[:, :D], both[:, D:] - erased[:, D:]], axis=1)
        direct = mm(twice(queries, 1), tall(prefix)) * jnp.exp(log_columns[:, c : c + 1])
        result = direct + mm3_wide(scores, residue)
        query_maps[c * CHUNK : (c + 1) * CHUNK, :] = wide(result[:, :D])
        base[c * CHUNK : (c + 1) * CHUNK, :] = result[:, D:]


def block_kernel(place, own, next_core, next_chip, across, before, total):
    odd, upper = place[0] % 2 == 1, place[0] >= 2
    low = jnp.where(odd, next_core[...], own[...]), jnp.where(odd, own[...], next_core[...])
    high = jnp.where(odd, across[...], next_chip[...]), jnp.where(odd, next_chip[...], across[...])
    block = [jnp.where(upper, b, a) for a, b in zip(low, high)]
    block += [jnp.where(upper, a, b) for a, b in zip(low, high)]
    eye = jnp.where(jnp.equal(*iotas(D, D)), 1.0, 0.0)
    prefix = jnp.concatenate([eye, jnp.zeros_like(eye)], axis=1)
    chosen = prefix
    for p in range(4):
        if p:
            chosen = jnp.where(place[0] == p, prefix, chosen)
        linear = block[p][:, :D]
        if p == 0:
            prefix = block[p].astype(F32)
        else:
            moved = mm(twice(linear, 1), tall(prefix))
            offset = block[p][:, D:].astype(F32)
            prefix = jnp.concatenate([moved[:, :D], moved[:, D:] + offset], axis=1)
    before[...] = chosen
    total[...] = prefix.astype(BF16)


def join_kernel(total, earlier, joined):
    moved = mm(total[:, :D], earlier[...])
    joined[:, :D] = moved[:, :D].astype(BF16)
    joined[:, D:] = (moved[:, D:] + total[:, D:].astype(F32)).astype(BF16)


def shift_kernel(before, earlier, query_maps, base, shifted_maps, shifted_base):
    first = before[...]
    moved = mm(wide(first[:, :D]), twice(earlier[...], 0))
    prefix = jnp.concatenate([moved[:, :D], moved[:, D:] + first[:, D:]], axis=1)
    high, low = split(prefix)
    for c in range(4):
        rows = slice(c * 256, (c + 1) * 256)
        maps = query_maps[rows, :]
        result = mm(maps, twice(high, 0)) + mm(maps[:, :D], low)
        shifted_maps[rows, :] = wide(result[:, :D])
        shifted_base[rows, :] = base[rows, :] + result[:, D:]


def output_kernel(near, far, farthest, query_maps, base, gain, sent):
    state = farthest[...].astype(F32)
    state = mm(twice(far[:, :D], 1), tall(state)) + far[:, D:].astype(F32)
    state = mm(twice(near[:, :D], 1), tall(state)) + near[:, D:].astype(F32)
    weights = square(state)
    for c in range(4):
        rows = slice(c * 256, (c + 1) * 256)
        core = halves(mm(query_maps[rows, :], weights)) + base[rows, :]
        scale = lax.rsqrt(jnp.mean(core * core, axis=1, keepdims=True) + 1e-06)
        sent[rows, :] = (core * scale * gain[...]).astype(BF16)


def unpack_kernel(received, out, rows):
    rows[...] = received[...].reshape(SLAB, D).astype(F32)
    for token in range(TOK):
        out[token] = rows[pl.ds(token, HEADS, stride=TOK), :].astype(BF16)


def call(kernel, outs, *operands, scratch=(), flops=0, scalars=0, raw=0):
    outs = [jax.ShapeDtypeStruct(shape, dtype) for shape, dtype in outs]
    size = sum(a.size * a.dtype.itemsize for a in operands)
    return pl.pallas_call(
        kernel,
        out_shape=outs if len(outs) > 1 else outs[0],
        in_specs=[SMEM] * scalars
        + [pl.BlockSpec(memory_space=pltpu.HBM)] * raw
        + [VMEM] * (len(operands) - scalars - raw),
        out_specs=[VMEM] * len(outs) if len(outs) > 1 else VMEM,
        scratch_shapes=scratch,
        compiler_params=pltpu.CompilerParams(vmem_limit_bytes=24 << 20),
        cost_estimate=pl.CostEstimate(flops=flops, bytes_accessed=size, transcendentals=0),
    )(*operands)


def local(queries, keys, values, log_decay, beta, norm_gain):
    sources = (log_decay.T, beta.T, norm_gain.reshape(1, D), keys, values, queries)
    packed, gains = call(
        pack_kernel,
        [((HEADS, ROWS, D), BF16), ((1, D), F32)],
        *(pltpu.with_memory_space_constraint(source, pltpu.HBM) for source in sources),
        scratch=[
            pltpu.VMEM((3, TOK, HEADS, D), BF16),
            pltpu.VMEM((HEADS, TOK), BF16),
            pltpu.VMEM((HEADS, TOK), BF16),
            pltpu.VMEM((3, SLAB, D), F32),
            pltpu.SemaphoreType.DMA((6,)),
        ],
        raw=6,
    )
    received = lax.all_to_all(packed, "head", 0, 0, tiled=True)
    maps, prefixes, solved = call(
        map_kernel,
        [((D, 2 * D), BF16), ((CHUNKS, D, 2 * D), F32), ((CHUNKS, CHUNK, 2 * D), F32)],
        received,
        flops=1 << 33,
    )
    count = lax.axis_size("seq")

    def swapped(bits):
        return lax.ppermute(maps, "seq", [(s, s ^ bits) for s in range(count)])

    block = [maps, swapped(1), swapped(2), swapped(3)]
    query_maps, base = call(
        query_kernel,
        [((SLAB, 2 * D), BF16), ((SLAB, D), F32)],
        received,
        prefixes,
        solved,
        flops=1 << 33,
    )
    place = (lax.axis_index("seq") % 4).astype(jnp.int32).reshape(1)
    before, total = call(
        block_kernel, [((D, 2 * D), F32), ((D, 2 * D), BF16)], place, *block, scalars=1
    )

    def moved(value, by):
        return lax.ppermute(value, "seq", [(s, s + by) for s in range(count - by)])

    earlier = moved(total, 4)
    joined = call(join_kernel, [((D, 2 * D), BF16)], total, earlier)
    near = moved(joined, 8)
    far = lax.ppermute(joined, "seq", [(s, (s ^ 2) + 16) for s in range(count - 16)])
    farthest = moved(joined[:, D:], 24)
    query_maps, base = call(
        shift_kernel,
        [((SLAB, 2 * D), BF16), ((SLAB, D), F32)],
        before,
        earlier,
        query_maps,
        base,
        flops=1 << 31,
    )
    normed = call(
        output_kernel,
        [((SLAB, D), BF16)],
        near,
        far,
        farthest,
        query_maps,
        base,
        gains,
    )
    returned = lax.all_to_all(normed.reshape(HEADS, TOK, D), "head", 0, 0, tiled=True)
    return call(unpack_kernel, [((TOK, HEADS, D), BF16)], returned, scratch=[pltpu.VMEM((SLAB, D), F32)])


def solution(mesh):
    rows = P(("seq", "head"), None, None)
    columns = P(("seq", "head"), None)
    return jax.shard_map(
        local,
        mesh=mesh,
        in_specs=(rows, rows, rows, columns, columns, P()),
        out_specs=rows,
        check_vma=False,
    )
```

```python
import jax
import jax.numpy as jnp
from jax import lax
from jax.experimental import pallas as pl
from jax.experimental.pallas import tpu as pltpu
from jax.sharding import PartitionSpec as P


D = 128
TOK = 64
HEADS = 16
SLAB = TOK * HEADS
CHUNK = 128
CHUNKS = SLAB // CHUNK
KEY, VALUE, QUERY, GATE, ROWS = 0, 64, 128, 192, 200
F32, BF16 = jnp.float32, jnp.bfloat16
VMEM = pl.BlockSpec(memory_space=pltpu.VMEM)
SMEM = pl.BlockSpec(memory_space=pltpu.SMEM)


def mm(left, right):
    return jnp.dot(left, right, preferred_element_type=F32)


def mm_nt(left, right):
    return lax.dot_general(left, right, (((1,), (1,)), ((), ())), preferred_element_type=F32)


def mm_tn(left, right):
    return lax.dot_general(left, right, (((0,), (0,)), ((), ())), preferred_element_type=F32)


def split(value):
    high = value.astype(BF16)
    return high, (value - high.astype(F32)).astype(BF16)


def wide(value):
    return jnp.concatenate(split(value), axis=1)


def tall(value):
    return jnp.concatenate(split(value), axis=0)


def twice(value, axis):
    return jnp.concatenate([value, value], axis=axis)


def square(value):
    high, low = split(value)
    top = jnp.concatenate([high, low], axis=1)
    bottom = jnp.concatenate([high, jnp.zeros_like(high)], axis=1)
    return jnp.concatenate([top, bottom], axis=0)


def halves(value):
    return value[:, :D] + value[:, D:]


def mm3(left, right):
    return halves(mm(wide(left), square(right)))


def mm3_wide(left, right):
    high, low = split(right)
    left_high, left_low = split(left)
    both = jnp.concatenate([left_high, left_low], axis=1)
    return mm(both, twice(high, 0)) + mm(left_high, low)


def iotas(rows, columns):
    shape = (rows, columns)
    return lax.broadcasted_iota(jnp.int32, shape, 0), lax.broadcasted_iota(jnp.int32, shape, 1)


def ones_where(condition):
    return jnp.where(condition, 1.0, 0.0).astype(BF16)


def gates(received):
    rows = received[:, GATE:ROWS, :].astype(F32)[:, 0, :].astype(BF16)
    chunk_ids, source_ids = iotas(CHUNKS, HEADS)
    even = mm(ones_where(source_ids == 2 * chunk_ids), rows).astype(BF16)
    odd = mm(ones_where(source_ids == 2 * chunk_ids + 1), rows).astype(BF16)
    to, at = iotas(CHUNK, D)
    sum_even = ones_where((at < TOK) & (at <= to))
    sum_odd = ones_where((at < TOK) & (at + TOK <= to))
    beta_even = ones_where((to < TOK) & (at == to + TOK))
    beta_odd = ones_where((to >= TOK) & (at == to))
    log_rows = mm_nt(even, sum_even) + mm_nt(odd, sum_odd)
    log_columns = mm_nt(sum_even, even) + mm_nt(sum_odd, odd)
    beta_rows = mm_nt(even, beta_even) + mm_nt(odd, beta_odd)
    beta_columns = mm_nt(beta_even, even) + mm_nt(beta_odd, odd)
    return log_rows, log_columns, beta_rows, beta_columns


def part(received, chunk, offset):
    return received[2 * chunk : 2 * chunk + 2, offset : offset + TOK, :].reshape(CHUNK, D)


def spread_of(log_rows, log_columns, chunk, row_ids, column_ids):
    difference = log_columns[:, chunk : chunk + 1] - log_rows[chunk : chunk + 1, :]
    return jnp.exp(jnp.where(row_ids >= column_ids, difference, -1e30))


def pack_kernel(*refs):
    sources, (sent, gains, taken, decays, betas, rows, arrived) = refs[:6], refs[6:]
    targets = (decays, betas, gains, taken.at[0], taken.at[1], taken.at[2])
    copies = [
        pltpu.make_async_copy(source, target, arrived.at[n])
        for n, (source, target) in enumerate(zip(sources, targets))
    ]
    for copy in copies:
        copy.start()
    for copy in copies[:3]:
        copy.wait()
    to, at = iotas(TOK, D)
    gate_rows = mm(decays[...], ones_where(at == to)) + mm(betas[...], ones_where(at == to + TOK))
    for head in range(HEADS):
        sent[head, GATE:ROWS, :] = jnp.broadcast_to(gate_rows[head : head + 1, :], (8, D)).astype(BF16)
    for n, offset in enumerate((KEY, VALUE, QUERY)):
        copies[3 + n].wait()
        raw = taken[n].reshape(SLAB, D).astype(F32)
        if n == 0:
            raw = raw * lax.rsqrt(jnp.sum(raw * raw, axis=1, keepdims=True) + 1e-06)
        rows[n] = raw
        for head in range(HEADS):
            picked = rows[n, pl.ds(head, TOK, stride=HEADS), :]
            sent[head, offset : offset + TOK, :] = picked.astype(BF16)


def map_kernel(received, sent, prefixes, solved):
    log_rows, log_columns, beta_rows, beta_columns = gates(received)
    row_ids, column_ids = iotas(CHUNK, CHUNK)
    apart = row_ids ^ column_ids
    eye = jnp.where(apart == 0, 1.0, 0.0)
    lowers, inverses = [], []
    for c in range(CHUNKS):
        keys = part(received, c, KEY)
        spread = spread_of(log_rows, log_columns, c, row_ids, column_ids)
        lower = jnp.where(row_ids > column_ids, mm_nt(keys, keys) * spread, 0.0)
        lower = lower * beta_columns[:, c : c + 1]
        lowers.append(lower)
        inverses.append(eye - jnp.where(apart == 1, lower, 0.0))
    for level in range(1, 7):
        mask = (apart >> level) == 1
        for c in range(CHUNKS):
            inverse = inverses[c]
            lower = jnp.where(mask, lowers[c], 0.0)
            if level < 4:
                inverse = inverse.astype(BF16)
                inner = mm(inverse, lower.astype(BF16)).astype(BF16)
                inverses[c] = inverses[c] - mm(inner, inverse)
            else:
                inverses[c] = inverse - mm3(mm3(inverse, lower), inverse)
    log_scale = jnp.exp(log_rows)
    prefix = None
    for c in range(CHUNKS):
        keys, values = part(received, c, KEY), part(received, c, VALUE)
        inverse = inverses[c] * beta_rows[c : c + 1, :]
        erasers = mm(wide(inverse * log_scale[c : c + 1, :]), twice(keys, 0))
        pseudo = mm(wide(inverse), twice(values, 0))
        both = jnp.concatenate([erasers, pseudo], axis=1)
        solved[c] = both
        last = log_rows[c : c + 1, CHUNK - 1 : CHUNK]
        carried = both * jnp.exp(last - log_columns[:, c : c + 1])
        maps = mm_tn(twice(keys, 0), tall(carried))
        linear = eye * jnp.exp(last) - maps[:, :D]
        offset = maps[:, D:]
        if prefix is None:
            prefixes[c] = jnp.concatenate([eye, jnp.zeros_like(eye)], axis=1)
            prefix = jnp.concatenate([linear, offset], axis=1)
        else:
            prefixes[c] = prefix
            moved = mm3_wide(linear, prefix)
            prefix = jnp.concatenate([moved[:, :D], moved[:, D:] + offset], axis=1)
    sent[...] = prefix.astype(BF16)


def query_kernel(received, prefixes, solved, query_maps, base):
    log_rows, log_columns, _, _ = gates(received)
    row_ids, column_ids = iotas(CHUNK, CHUNK)
    for c in range(CHUNKS):
        keys = part(received, c, KEY)
        raw = part(received, c, QUERY).astype(F32)
        total = jnp.sum(raw * raw, axis=1, keepdims=True)
        queries = (raw * lax.rsqrt(total + 1e-06) * D**-0.5).astype(BF16)
        spread = spread_of(log_rows, log_columns, c, row_ids, column_ids)
        scores = mm_nt(queries, keys) * spread
        prefix, both = prefixes[c], solved[c]
        erased = mm3_wide(both[:, :D], prefix)
        residue = jnp.concatenate([-erased[:, :D], both[:, D:] - erased[:, D:]], axis=1)
        direct = mm(twice(queries, 1), tall(prefix)) * jnp.exp(log_columns[:, c : c + 1])
        result = direct + mm3_wide(scores, residue)
        query_maps[c * CHUNK : (c + 1) * CHUNK, :] = wide(result[:, :D])
        base[c * CHUNK : (c + 1) * CHUNK, :] = result[:, D:]


def block_kernel(place, own, next_core, next_chip, across, before, total):
    odd, upper = place[0] % 2 == 1, place[0] >= 2
    low = jnp.where(odd, next_core[...], own[...]), jnp.where(odd, own[...], next_core[...])
    high = jnp.where(odd, across[...], next_chip[...]), jnp.where(odd, next_chip[...], across[...])
    block = [jnp.where(upper, b, a) for a, b in zip(low, high)]
    block += [jnp.where(upper, a, b) for a, b in zip(low, high)]
    eye = jnp.where(jnp.equal(*iotas(D, D)), 1.0, 0.0)
    prefix = jnp.concatenate([eye, jnp.zeros_like(eye)], axis=1)
    chosen = prefix
    for p in range(4):
        if p:
            chosen = jnp.where(place[0] == p, prefix, chosen)
        linear = block[p][:, :D]
        if p == 0:
            prefix = block[p].astype(F32)
        else:
            moved = mm(twice(linear, 1), tall(prefix))
            offset = block[p][:, D:].astype(F32)
            prefix = jnp.concatenate([moved[:, :D], moved[:, D:] + offset], axis=1)
    before[...] = chosen
    total[...] = prefix.astype(BF16)


def join_kernel(total, earlier, joined):
    moved = mm(total[:, :D], earlier[...])
    joined[:, :D] = moved[:, :D].astype(BF16)
    joined[:, D:] = (moved[:, D:] + total[:, D:].astype(F32)).astype(BF16)


def shift_kernel(before, earlier, query_maps, base, shifted_maps, shifted_base):
    first = before[...]
    moved = mm(wide(first[:, :D]), twice(earlier[...], 0))
    prefix = jnp.concatenate([moved[:, :D], moved[:, D:] + first[:, D:]], axis=1)
    high, low = split(prefix)
    for c in range(4):
        rows = slice(c * 256, (c + 1) * 256)
        maps = query_maps[rows, :]
        result = mm(maps, twice(high, 0)) + mm(maps[:, :D], low)
        shifted_maps[rows, :] = wide(result[:, :D])
        shifted_base[rows, :] = base[rows, :] + result[:, D:]


def output_kernel(near, far, farthest, query_maps, base, gain, sent):
    state = farthest[...].astype(F32)
    state = mm(twice(far[:, :D], 1), tall(state)) + far[:, D:].astype(F32)
    state = mm(twice(near[:, :D], 1), tall(state)) + near[:, D:].astype(F32)
    weights = square(state)
    for c in range(4):
        rows = slice(c * 256, (c + 1) * 256)
        core = halves(mm(query_maps[rows, :], weights)) + base[rows, :]
        scale = lax.rsqrt(jnp.mean(core * core, axis=1, keepdims=True) + 1e-06)
        sent[rows, :] = (core * scale * gain[...]).astype(BF16)


def unpack_kernel(received, out, rows):
    rows[...] = received[...].reshape(SLAB, D).astype(F32)
    for token in range(TOK):
        out[token] = rows[pl.ds(token, HEADS, stride=TOK), :].astype(BF16)


def call(kernel, outs, *operands, scratch=(), flops=0, scalars=0, raw=0):
    outs = [jax.ShapeDtypeStruct(shape, dtype) for shape, dtype in outs]
    size = sum(a.size * a.dtype.itemsize for a in operands)
    return pl.pallas_call(
        kernel,
        out_shape=outs if len(outs) > 1 else outs[0],
        in_specs=[SMEM] * scalars
        + [pl.BlockSpec(memory_space=pltpu.HBM)] * raw
        + [VMEM] * (len(operands) - scalars - raw),
        out_specs=[VMEM] * len(outs) if len(outs) > 1 else VMEM,
        scratch_shapes=scratch,
        compiler_params=pltpu.CompilerParams(vmem_limit_bytes=24 << 20),
        cost_estimate=pl.CostEstimate(flops=flops, bytes_accessed=size, transcendentals=0),
    )(*operands)


def local(queries, keys, values, log_decay, beta, norm_gain):
    sources = (log_decay.T, beta.T, norm_gain.reshape(1, D), keys, values, queries)
    packed, gains = call(
        pack_kernel,
        [((HEADS, ROWS, D), BF16), ((1, D), F32)],
        *(pltpu.with_memory_space_constraint(source, pltpu.HBM) for source in sources),
        scratch=[
            pltpu.VMEM((3, TOK, HEADS, D), BF16),
            pltpu.VMEM((HEADS, TOK), BF16),
            pltpu.VMEM((HEADS, TOK), BF16),
            pltpu.VMEM((3, SLAB, D), F32),
            pltpu.SemaphoreType.DMA((6,)),
        ],
        raw=6,
    )
    received = lax.all_to_all(packed, "head", 0, 0, tiled=True)
    maps, prefixes, solved = call(
        map_kernel,
        [((D, 2 * D), BF16), ((CHUNKS, D, 2 * D), F32), ((CHUNKS, CHUNK, 2 * D), F32)],
        received,
        flops=1 << 33,
    )
    count = lax.axis_size("seq")

    def swapped(bits):
        return lax.ppermute(maps, "seq", [(s, s ^ bits) for s in range(count)])

    block = [maps, swapped(1), swapped(2), swapped(3)]
    query_maps, base = call(
        query_kernel,
        [((SLAB, 2 * D), BF16), ((SLAB, D), F32)],
        received,
        prefixes,
        solved,
        flops=1 << 33,
    )
    place = (lax.axis_index("seq") % 4).astype(jnp.int32).reshape(1)
    before, total = call(
        block_kernel, [((D, 2 * D), F32), ((D, 2 * D), BF16)], place, *block, scalars=1
    )

    def moved(value, by):
        return lax.ppermute(value, "seq", [(s, s + by) for s in range(count - by)])

    earlier = moved(total, 4)
    joined = call(join_kernel, [((D, 2 * D), BF16)], total, earlier)
    near = moved(joined, 8)
    far = lax.ppermute(joined, "seq", [(s, (s ^ 2) + 16) for s in range(count - 16)])
    farthest = moved(joined[:, D:], 24)
    query_maps, base = call(
        shift_kernel,
        [((SLAB, 2 * D), BF16), ((SLAB, D), F32)],
        before,
        earlier,
        query_maps,
        base,
        flops=1 << 31,
    )
    normed = call(
        output_kernel,
        [((SLAB, D), BF16)],
        near,
        far,
        farthest,
        query_maps,
        base,
        gains,
    )
    returned = lax.all_to_all(normed.reshape(HEADS, TOK, D), "head", 0, 0, tiled=True)
    return call(unpack_kernel, [((TOK, HEADS, D), BF16)], returned, scratch=[pltpu.VMEM((SLAB, D), F32)])


def solution(mesh):
    rows = P(("seq", "head"), None, None)
    columns = P(("seq", "head"), None)
    return jax.shard_map(
        local,
        mesh=mesh,
        in_specs=(rows, rows, rows, columns, columns, P()),
        out_specs=rows,
        check_vma=False,
    )
```
